512 devices in a mesh: leaf: 128 (over z, y, core), list: 4 (over x).
Axes of the slice: x: 4, y: 8, z: 8, core: 2. Of those that a mesh axis runs over, the one named last changes fastest.
Arguments:
- points: bfloat16 [32, 524288], P(None, 'leaf')
- charges: bfloat16 [32, 524288], P(None, 'leaf'), may hold values from -0.59765625 to 0.59765625
- leaf_ids: int32 [2048, 128], P('leaf'), may hold values from 0 to 255, as said below
- inner_ids: int32 [1920, 128], P('leaf'), may hold values from 0 to 255, as said below
- upper_ids_first: int32 [64, 128], replicated, may hold values from 0 to 255, as said below
- upper_ids_second: int32 [32, 128], replicated, may hold values from 0 to 255, as said below
- upper_ids_third: int32 [16, 128], replicated, may hold values from 0 to 255, as said below
- leaf_maps: bfloat16 [2048, 128, 256], P('leaf'), may hold values from -0.375 to 0.375
- inner_maps: bfloat16 [1920, 128, 256], P('leaf'), may hold values from -0.4375 to 0.4375
- upper_maps_first: bfloat16 [8192, 256], P('leaf'), may hold values from -0.4375 to 0.4375
- upper_maps_second: bfloat16 [4096, 256], P('leaf'), may hold values from -0.4375 to 0.4375
- upper_maps_third: bfloat16 [2048, 256], P('leaf'), may hold values from -0.4375 to 0.4375
- near_lists: int32 [2048, 32], P('leaf', 'list'), may hold values from -1 to 2047, as said below
- far_inner: int32 [3968, 32], P('leaf', 'list'), may hold values from 0 to 2047, as said below
- far_upper_first: int32 [64, 32], P(None, 'list'), may hold values from 0 to 63
- far_upper_second: int32 [32, 32], P(None, 'list'), may hold values from 0 to 31
- far_upper_third: int32 [16, 32], P(None, 'list'), may hold values from 0 to 15
Outputs:
- potentials: float32 [32, 524288], P(None, ('leaf', 'list'))
The draws below stay inside these ranges and needn't reach their ends.
Inputs may be any that keep to these rules, and one draw needn't show every extreme that they name: `leaf_ids`: each row holds 128 distinct columns of its leaf. `inner_ids`: each row holds 128 distinct columns of its node's 2 * 128 child skeleton columns. `upper_ids_first`: each row holds 128 distinct columns of its node's 2 * 128 child skeleton columns. `upper_ids_second`: each row holds 128 distinct columns of its node's 2 * 128 child skeleton columns. `upper_ids_third`: each row holds 128 distinct columns of its node's 2 * 128 child skeleton columns. `near_lists`: each row starts with one or more leaf numbers and is -1 after them; some row has 32 leaf numbers. A leaf number s in row i satisfies |s // 16 - i // 16| <= 1. `far_inner`: an entry s of node i at level l satisfies |s // (16 >> l) - i // (16 >> l)| <= 1, both numbered within level l.
All inputs are finite; a program needn't handle non-finite values.
Results may differ from the reference program's by a relative error of at most 0.01.
Values may be sent and summed in bfloat16 or wider, within the bound.
A program may use at most 128 MiB of HBM per device.

```python
import jax
import jax.numpy as jnp
from jax import lax

DIM = 32
LEAF = 256
SKEL = 128
RHS = 32
NEAR = 32
FAR = 32
LOCAL = 4
LEAF_DEV = 16
SUBTREES = 128
LEAVES = 2048
POINTS = 524288


def draw_points(key, part):
    key_centre, key_spread = jax.random.split(key)
    centres = 0.5 * jax.random.normal(key_centre, (DIM, LEAVES, 1))
    spread = 0.55 * jax.random.normal(key_spread, (DIM, LEAVES, LEAF))
    return (centres + spread).reshape(DIM, POINTS).astype(jnp.bfloat16)


def distinct_prefix(key, row_count, choose_from, keep_count):
    scores = jax.random.randint(key, (row_count, choose_from), 0, 1 << 20) * choose_from
    scores = scores + jnp.arange(choose_from, dtype=jnp.int32)[None, :]
    return jnp.argsort(scores, axis=1, stable=True)[:, :keep_count].astype(jnp.int32)


def draw_leaf_ids(key, part):
    return distinct_prefix(jax.random.fold_in(key, 11), LEAVES, LEAF, SKEL)


def draw_inner_ids(key, part):
    return distinct_prefix(jax.random.fold_in(key, 12), SUBTREES * (LEAF_DEV - 1), 2 * SKEL, SKEL)


def draw_upper_ids_first(key, part):
    return distinct_prefix(jax.random.fold_in(key, 13), SUBTREES // 2, 2 * SKEL, SKEL)


def draw_upper_ids_second(key, part):
    return distinct_prefix(jax.random.fold_in(key, 14), SUBTREES // 4, 2 * SKEL, SKEL)


def draw_upper_ids_third(key, part):
    return distinct_prefix(jax.random.fold_in(key, 15), SUBTREES // 8, 2 * SKEL, SKEL)


def draw_near_lists(key, part):
    key_count, key_side, key_within = jax.random.split(jax.random.fold_in(key, 16), 3)
    leaf_index = jnp.arange(LEAVES, dtype=jnp.int32)
    counts = jax.random.randint(key_count, (LEAVES,), 1, NEAR + 1).at[0].set(NEAR)
    neighbour_side = jax.random.randint(key_side, (LEAVES, NEAR), -1, 2)
    subtree = jnp.clip(leaf_index[:, None] // LEAF_DEV + neighbour_side, 0, SUBTREES - 1)
    within = jax.random.randint(key_within, (LEAVES, NEAR), 0, LEAF_DEV)
    entries = subtree * LEAF_DEV + within
    slot_index = jnp.arange(NEAR, dtype=jnp.int32)
    return jnp.where(slot_index[None, :] < counts[:, None], entries, -1).astype(jnp.int32)


def draw_far_inner(key, part):
    blocks = []
    for degree in range(LOCAL + 1):
        per_tree = LEAF_DEV >> degree
        key_side, key_within = jax.random.split(jax.random.fold_in(key, 100 + degree))
        home_tree = jnp.arange(SUBTREES, dtype=jnp.int32)[:, None, None]
        neighbour_side = jax.random.randint(key_side, (SUBTREES, per_tree, FAR), -1, 2)
        target_tree = jnp.clip(home_tree + neighbour_side, 0, SUBTREES - 1)
        within = jax.random.randint(key_within, (SUBTREES, per_tree, FAR), 0, per_tree)
        blocks.append(target_tree * per_tree + within)
    return jnp.concatenate(blocks, axis=1).reshape(SUBTREES * (2 * LEAF_DEV - 1), FAR).astype(jnp.int32)


def plant(values, stream_key, least, largest):
    longest = values.shape.index(max(values.shape))
    spots = []
    for shift in (0, 1):
        where = [jax.random.randint(jax.random.fold_in(stream_key, axis), (), 0, length) for axis, length in enumerate(values.shape)]
        where[longest] = (where[longest] + shift) % values.shape[longest]
        spots.append(tuple(where))
    return values.at[spots[0]].set(least).at[spots[1]].set(largest)


def levels(key, dims, shards, low, top_value):
    level, own = 1.0, jax.random.fold_in(key, 6)
    for position, shards_of in shards:
        draws = jnp.exp(jax.random.uniform(jax.random.fold_in(own, position), (shards_of,), jnp.float32, low / len(shards), top_value / len(shards)))
        level = level * jnp.repeat(draws, dims[position] // shards_of).reshape([-1 if axis == position else 1 for axis in range(len(dims))])
    return level


def noise(stream_key, dims, scale, reach, shards=(), kind=jnp.bfloat16):
    array = scale * jax.random.normal(stream_key, dims, jnp.float32)
    if shards:
        array = array * levels(stream_key, dims, shards, -0.22, 0.18)
    return jnp.clip(array, -reach, reach).astype(kind)


def setup_inputs(seed: int = 0) -> dict:
    streams_of = jax.random.split(jax.random.key(seed), 18)
    return {
        "points": draw_points(jax.random.fold_in(streams_of[17], 71), 0),
        "charges": noise(streams_of[1], (RHS, POINTS), 0.1, 0.59765625, ((1, 128),)),
        "leaf_ids": draw_leaf_ids(jax.random.fold_in(streams_of[17], 71), 0),
        "inner_ids": draw_inner_ids(jax.random.fold_in(streams_of[17], 71), 0),
        "upper_ids_first": draw_upper_ids_first(jax.random.fold_in(streams_of[17], 71), 0),
        "upper_ids_second": draw_upper_ids_second(jax.random.fold_in(streams_of[17], 71), 0),
        "upper_ids_third": draw_upper_ids_third(jax.random.fold_in(streams_of[17], 71), 0),
        "leaf_maps": noise(streams_of[7], (LEAVES, SKEL, LEAF), LEAF ** -0.5, 0.375, ((0, 128),)),
        "inner_maps": noise(streams_of[8], (SUBTREES * (LEAF_DEV - 1), SKEL, 2 * SKEL), (3 * SKEL // 2) ** -0.5, 0.4375, ((0, 128),)),
        "upper_maps_first": noise(streams_of[9], (SUBTREES // 2 * SKEL, 2 * SKEL), (3 * SKEL // 2) ** -0.5, 0.4375, ((0, 128),)),
        "upper_maps_second": noise(streams_of[10], (SUBTREES // 4 * SKEL, 2 * SKEL), (3 * SKEL // 2) ** -0.5, 0.4375, ((0, 128),)),
        "upper_maps_third": noise(streams_of[11], (SUBTREES // 8 * SKEL, 2 * SKEL), (3 * SKEL // 2) ** -0.5, 0.4375, ((0, 128),)),
        "near_lists": draw_near_lists(jax.random.fold_in(streams_of[17], 71), 0),
        "far_inner": draw_far_inner(jax.random.fold_in(streams_of[17], 71), 0),
        "far_upper_first": plant(jax.random.randint(streams_of[14], (SUBTREES // 2, FAR), 0, SUBTREES // 2), jax.random.fold_in(streams_of[14], 1), 0, (SUBTREES // 2) - 1).astype(jnp.int32),
        "far_upper_second": plant(jax.random.randint(streams_of[15], (SUBTREES // 4, FAR), 0, SUBTREES // 4), jax.random.fold_in(streams_of[15], 1), 0, (SUBTREES // 4) - 1).astype(jnp.int32),
        "far_upper_third": plant(jax.random.randint(streams_of[16], (SUBTREES // 8, FAR), 0, SUBTREES // 8), jax.random.fold_in(streams_of[16], 1), 0, (SUBTREES // 8) - 1).astype(jnp.int32),
    }


def kernel_from(goal_coords, source_coords):
    goal_wide = goal_coords.astype(jnp.float32)
    source_wide = source_coords.astype(jnp.float32)
    goal_norm = jnp.sum(goal_wide * goal_wide, axis=-2)
    source_norm = jnp.sum(source_wide * source_wide, axis=-2)
    cross = jnp.einsum("...da,...db->...ab", goal_wide, source_wide, precision=lax.Precision.HIGHEST)
    distance = goal_norm[..., :, None] + source_norm[..., None, :] - 2.0 * cross
    return jnp.exp(distance * (-3.0 / DIM)).astype(jnp.bfloat16)


def near_field(grid_points, grid_charges, near_lists):
    def one_leaf(leaf_index):
        entries = lax.dynamic_index_in_dim(near_lists, leaf_index, 0, keepdims=False)
        is_live = entries >= 0
        safe_entries = jnp.where(is_live, entries, 0).astype(jnp.int32)
        source_coords = jnp.take(grid_points, safe_entries, axis=1).transpose(1, 0, 2)
        source_loads = jnp.take(grid_charges, safe_entries, axis=1)
        goal_coords = lax.dynamic_index_in_dim(grid_points, leaf_index, 1, keepdims=False)
        goal_coords = jnp.broadcast_to(goal_coords[None], source_coords.shape)
        kernel = kernel_from(goal_coords, source_coords) * is_live[:, None, None].astype(jnp.bfloat16)
        return jnp.einsum("rnb,nab->ra", source_loads.astype(jnp.float32), kernel.astype(jnp.float32),
                          precision=lax.Precision.HIGHEST)

    return lax.map(one_leaf, jnp.arange(LEAVES, dtype=jnp.int32))


def far_field(coords, weights, lists):
    def one_node(node_index):
        entries = lax.dynamic_index_in_dim(lists, node_index, 0, keepdims=False)
        source_coords = jnp.take(coords, entries, axis=0)
        source_loads = jnp.take(weights, entries, axis=0)
        goal_coords = lax.dynamic_index_in_dim(coords, node_index, 0, keepdims=False)
        goal_coords = jnp.broadcast_to(goal_coords[None], source_coords.shape)
        kernel = kernel_from(goal_coords, source_coords)
        return jnp.einsum("frs,fts->rt", source_loads.astype(jnp.float32), kernel.astype(jnp.float32),
                          precision=lax.Precision.HIGHEST)

    return lax.map(one_node, jnp.arange(coords.shape[0], dtype=jnp.int32))


def climb_level(coords, weights, chosen, matrices):
    parents = coords.shape[0] // 2
    joined_coords = coords.reshape(parents, 2, DIM, SKEL).transpose(0, 2, 1, 3).reshape(parents, DIM, 2 * SKEL)
    joined_loads = weights.reshape(parents, 2, RHS, SKEL).transpose(0, 2, 1, 3).reshape(parents, RHS, 2 * SKEL)
    new_coords = jnp.take_along_axis(joined_coords, chosen[:, None, :], axis=2)
    new_loads = jnp.einsum("nrk,nsk->nrs", joined_loads.astype(jnp.float32), matrices.astype(jnp.float32),
                           precision=lax.Precision.HIGHEST).astype(jnp.bfloat16)
    return new_coords, new_loads


def reference(points, charges, leaf_ids, inner_ids, upper_ids_first, upper_ids_second, upper_ids_third,
              leaf_maps, inner_maps, upper_maps_first, upper_maps_second, upper_maps_third,
              near_lists, far_inner, far_upper_first, far_upper_second, far_upper_third):
    grid_points = points.reshape(DIM, LEAVES, LEAF)
    grid_charges = charges.reshape(RHS, LEAVES, LEAF)
    coords_list = [jnp.take_along_axis(grid_points, leaf_ids[None], axis=2).transpose(1, 0, 2)]
    weights_list = [jnp.einsum("rnp,nsp->nrs", grid_charges.astype(jnp.float32), leaf_maps.astype(jnp.float32),
                               precision=lax.Precision.HIGHEST).astype(jnp.bfloat16)]
    inner_rows = inner_ids.reshape(SUBTREES, LEAF_DEV - 1, SKEL)
    inner_mats = inner_maps.reshape(SUBTREES, LEAF_DEV - 1, SKEL, 2 * SKEL)
    far_rows = far_inner.reshape(SUBTREES, 2 * LEAF_DEV - 1, FAR)
    lists_all = []
    maps_all = []
    for degree in range(LOCAL + 1):
        per_tree = LEAF_DEV >> degree
        offset_row = 2 * LEAF_DEV - 2 * per_tree
        lists_all.append(far_rows[:, offset_row:offset_row + per_tree].reshape(-1, FAR))
    for degree in range(1, LOCAL + 1):
        per_tree = LEAF_DEV >> degree
        offset_row = LEAF_DEV - 2 * per_tree
        chosen = inner_rows[:, offset_row:offset_row + per_tree].reshape(-1, SKEL)
        matrices = inner_mats[:, offset_row:offset_row + per_tree].reshape(-1, SKEL, 2 * SKEL)
        maps_all.append(matrices)
        new_coords, new_loads = climb_level(coords_list[-1], weights_list[-1], chosen, matrices)
        coords_list.append(new_coords)
        weights_list.append(new_loads)
    uppers = ((upper_ids_first, upper_maps_first, far_upper_first),
              (upper_ids_second, upper_maps_second, far_upper_second),
              (upper_ids_third, upper_maps_third, far_upper_third))
    for chosen, flat_maps, far_list in uppers:
        matrices = flat_maps.reshape(-1, SKEL, 2 * SKEL)
        maps_all.append(matrices)
        lists_all.append(far_list)
        new_coords, new_loads = climb_level(coords_list[-1], weights_list[-1], chosen, matrices)
        coords_list.append(new_coords)
        weights_list.append(new_loads)
    far_terms = [far_field(coords_list[degree], weights_list[degree], lists_all[degree])
                 for degree in range(len(coords_list))]
    totals = far_terms[-1]
    for degree in range(len(far_terms) - 1, 0, -1):
        spread = jnp.einsum("nrs,nsk->nrk", totals, maps_all[degree - 1].astype(jnp.float32),
                            precision=lax.Precision.HIGHEST)
        parents = spread.shape[0]
        children = spread.reshape(parents, RHS, 2, SKEL).transpose(0, 2, 1, 3).reshape(2 * parents, RHS, SKEL)
        totals = far_terms[degree - 1] + children
    far_leaf = jnp.einsum("nrs,nsp->nrp", totals, leaf_maps.astype(jnp.float32), precision=lax.Precision.HIGHEST)
    near_part = near_field(grid_points, grid_charges, near_lists)
    return (near_part + far_leaf).transpose(1, 0, 2).reshape(RHS, POINTS)
```

```python
import functools
import math

import jax
import jax.numpy as jnp
from jax import lax
from jax.experimental import pallas as pl
from jax.experimental.pallas import tpu as pltpu
from jax.sharding import PartitionSpec as P

MESH = pl.DeviceIdType.MESH
BF16 = jnp.bfloat16
F32 = jnp.float32
VMEM = pl.BlockSpec(memory_space=pltpu.VMEM)
SMEM = pl.BlockSpec(memory_space=pltpu.SMEM)
UNROLL = 4
NODES = 31
OFFSETS = (0, 16, 24, 28, 30)
RATE = -3.0 / 32.0 * math.log2(math.e)
NT = (((1,), (1,)), ((), ()))


def dot(a, b):
    return jnp.dot(a, b, preferred_element_type=F32)


def dot_nt(a, b):
    return lax.dot_general(a, b, NT, preferred_element_type=F32)


def climb(pair, ids, mat):
    rows = lax.broadcasted_iota(jnp.int32, (256, 128), 0)
    hot = jnp.where(rows == ids, 1.0, 0.0).astype(BF16)
    coords = dot(pair[:32], hot).astype(BF16)
    weights = dot_nt(pair[32:], mat).astype(BF16)
    return coords, weights


def gather_kernel(
    points, charges, leaf_ids, inner_ids, ids5, ids6, ids7, leaf_maps, inner_maps,
    maps5, maps6, maps7, near, far5, far6, far7,
    side_points, side_charges, nodes, side_nodes, all5, all6, all7, near_all, own_upper, chosen,
    roots, group5, group6, group7, half5, half6, half7, sent, buf5, buf6, buf7,
    map_send, map_recv, list_send, list_recv, root_send, root_recv, side_send, side_recv,
    ring_send, ring_recv, swap_send, swap_recv,
):
    leaf = lax.axis_index("leaf")
    plane = lax.axis_index("list")
    core = leaf % 2
    y = (leaf // 2) % 8
    z = leaf // 16
    g = leaf % 8
    base8 = leaf - g
    sides = ((leaf + 127) % 128, (leaf + 1) % 128)
    group = [base8 + (g + k) % 8 for k in range(1, 8)]
    row = [z * 16 + ((y + k) % 8) * 2 + core for k in range(1, 8)]
    column = [((z + k) % 8) * 16 + y * 2 + core for k in range(1, 8)]
    sibling = leaf + 1 - 2 * core

    def to(who):
        return (who, plane)

    barrier = pltpu.get_barrier_semaphore()
    peers = [to(w) for w in (*sides, *group, *row, *column)]
    peers += [(leaf, (plane + k) % 4) for k in range(1, 4)]
    for who in peers:
        pl.semaphore_signal(barrier, inc=1, device_id=who, device_id_type=MESH)
    pl.semaphore_wait(barrier, len(peers))

    copies = []

    def send(src, dst, s_sem, r_sem, who):
        copy = pltpu.make_async_remote_copy(
            src_ref=src, dst_ref=dst, send_sem=s_sem, recv_sem=r_sem, device_id=who, device_id_type=MESH
        )
        copy.start()
        copies.append(copy)
        return copy

    map_copies = []
    for k in range(1, 8):
        for level, (src, dst) in enumerate(((maps5, all5), (maps6, all6), (maps7, all7))):
            map_copies.append(
                send(src, dst.at[g], map_send.at[level, k], map_recv.at[level, k], to(group[k - 1]))
            )
    list_copies = [
        send(near, near_all.at[plane], list_send.at[k], list_recv.at[k], (leaf, (plane + k) % 4))
        for k in range(1, 4)
    ]
    all5[g] = maps5[...]
    all6[g] = maps6[...]
    all7[g] = maps7[...]
    near_all[plane] = near[...]

    for i in range(16):
        cols = slice(i * 256, (i + 1) * 256)
        pair = jnp.concatenate([points[:, cols], charges[:, cols]], axis=0)
        coords, weights = climb(pair, leaf_ids[i : i + 1, :], leaf_maps[i])
        nodes[i, :32] = coords
        nodes[i, 32:] = weights
    for level in range(1, 5):
        for i in range(16 >> level):
            child = OFFSETS[level - 1] + 2 * i
            here = OFFSETS[level] + i
            pair = jnp.concatenate([nodes[child], nodes[child + 1]], axis=1)
            coords, weights = climb(pair, inner_ids[here - 16 : here - 15, :], inner_maps[here - 16])
            nodes[here, :32] = coords
            nodes[here, 32:] = weights
    roots[g] = nodes[30]

    root_copies = [
        send(roots.at[g], roots.at[g], root_send.at[k], root_recv.at[k], to(group[k - 1]))
        for k in range(1, 8)
    ]
    side_copies = []
    for way in range(2):
        dst = 1 - way
        for n, (src, out) in enumerate(
            ((nodes, side_nodes), (points, side_points), (charges, side_charges))
        ):
            side_copies.append(
                send(src, out.at[dst], side_send.at[way, n], side_recv.at[way, n], to(sides[way]))
            )

    for copy in map_copies + root_copies:
        copy.wait_recv()

    def keep(dst, j, coords, weights):
        dst[j, :32] = coords
        dst[j, 32:] = weights

    quad = leaf // 8
    for j in range(4):
        pair = jnp.concatenate([roots[2 * j], roots[2 * j + 1]], axis=1)
        mat = jnp.concatenate([all5[2 * j], all5[2 * j + 1]], axis=0)
        keep(group5, j, *climb(pair, ids5[pl.ds(quad * 4 + j, 1), :], mat))
    for j in range(2):
        pair = jnp.concatenate([group5[2 * j], group5[2 * j + 1]], axis=1)
        mat = jnp.concatenate([all6[4 * j + n] for n in range(4)], axis=0)
        keep(group6, j, *climb(pair, ids6[pl.ds(quad * 2 + j, 1), :], mat))
    pair = jnp.concatenate([group6[0], group6[1]], axis=1)
    mat = jnp.concatenate([all7[n] for n in range(8)], axis=0)
    keep(group7, 0, *climb(pair, ids7[pl.ds(quad, 1), :], mat))

    mine = (group5[g // 2], group6[g // 4], group7[0])
    halves = (half5, half6, half7)
    for level in range(3):
        own_upper[level] = mine[level][:32]

    def put_half(c):
        for level in range(3):
            halves[level][:16] = mine[level][16 * c : 16 * c + 16]
            halves[level][16:] = mine[level][32 + 16 * c : 48 + 16 * c]

    @pl.when(core == 0)
    def _():
        put_half(0)
        slots = (leaf // 2, leaf // 4, leaf // 8)
        bufs = (buf5, buf6, buf7)
        ks = (range(1, 8), (2, 4, 6), (4,))
        first = []
        for level in range(3):
            for k in ks[level]:
                first.append(
                    send(
                        halves[level], bufs[level].at[slots[level]],
                        ring_send.at[0, level, k], ring_recv.at[0, level, k], to(row[k - 1]),
                    )
                )
            bufs[level][slots[level]] = halves[level][...]
        second = []
        for level in range(3):
            for copy in first:
                pass
        at = 0
        for level in range(3):
            for _k in ks[level]:
                first[at].wait_recv()
                at += 1
            size = 8 >> level
            slab = bufs[level].at[pl.ds(z * size, size)]
            for k in range(1, 8):
                second.append(
                    send(slab, slab, ring_send.at[1, level, k], ring_recv.at[1, level, k], to(column[k - 1]))
                )
        for copy in second:
            copy.wait_recv()
        for copy in first + second:
            copy.wait_send()

    @pl.when(core == 1)
    def _():
        put_half(1)
        slots = (y * 8 + z, (y // 2) * 8 + z, (y // 4) * 8 + z)
        bufs = (buf5, buf6, buf7)
        ks = (range(1, 8), (2, 4, 6), (4,))
        first = []
        for level in range(3):
            for k in range(1, 8):
                first.append(
                    send(
                        halves[level], bufs[level].at[slots[level]],
                        ring_send.at[0, level, k], ring_recv.at[0, level, k], to(column[k - 1]),
                    )
                )
            bufs[level][slots[level]] = halves[level][...]
        second = []
        for level in range(3):
            for k in range(7):
                first[level * 7 + k].wait_recv()
            slab = bufs[level].at[pl.ds((y // (1 << level)) * 8, 8)]
            for k in ks[level]:
                second.append(
                    send(slab, slab, ring_send.at[1, level, k], ring_recv.at[1, level, k], to(row[k - 1]))
                )
        for copy in second:
            copy.wait_recv()
        for copy in first + second:
            copy.wait_send()

    for f in range(8):
        n5 = far5[leaf // 2, f]
        n6 = far6[leaf // 4, f]
        n7 = far7[leaf // 8, f]
        sent[f] = buf5[(1 - core) * n5 + core * ((n5 % 8) * 8 + n5 // 8)]
        sent[8 + f] = buf6[(1 - core) * n6 + core * ((n6 % 4) * 8 + n6 // 4)]
        sent[16 + f] = buf7[(1 - core) * n7 + core * ((n7 % 2) * 8 + n7 // 2)]
    swap = send(sent, chosen.at[core], swap_send, swap_recv, to(sibling))
    chosen[core] = sent[...]
    swap.wait_recv()
    for copy in side_copies + list_copies:
        copy.wait_recv()
    for copy in map_copies + list_copies + root_copies + side_copies + [swap]:
        copy.wait_send()


def extra_rows(coords, target):
    wide = coords.astype(F32)
    norm = jnp.sum(wide * wide, axis=0, keepdims=True)
    high = norm.astype(BF16).astype(F32)
    rest = norm - high
    middle = rest.astype(BF16).astype(F32)
    low = (rest - middle).astype(BF16).astype(F32)
    shape = (16, coords.shape[1])
    row = lax.broadcasted_iota(jnp.int32, shape, 0)
    at, ones = (3, 0) if target else (0, 3)
    out = jnp.where((row >= ones) & (row < ones + 3), 1.0, 0.0)
    for n, part in enumerate((high, middle, low)):
        out = jnp.where(row == at + n, jnp.broadcast_to(part, shape), out)
    return out


def turned(coords):
    width = coords.shape[1]
    rows = [-2.0 * coords.astype(F32), extra_rows(coords, True), jnp.zeros((80, width), F32)]
    return jnp.concatenate(rows, axis=0).T.astype(BF16)


def field_kernel(
    points, charges, side_points, side_charges, nodes, side_nodes, all5, all6, all7,
    own_upper, chosen, inner_maps, leaf_maps, near_all, far_inner,
    out,
    leaf_block, node_block, leaf_turned, node_turned, near_sum, far_sum, source, owner, table,
):
    leaf = lax.axis_index("leaf")
    plane = lax.axis_index("list")
    g = leaf % 8

    def list_pair(t, count):
        i = t // 8
        slot = 4 * (t % 8) + (plane + i) % 4
        entry = near_all[(slot // 8) * 16 + i, slot % 8]
        source[count] = entry - (leaf - 1) * 16
        owner[count] = i
        return count + jnp.where(entry >= 0, 1, 0)

    live = lax.fori_loop(0, 128, list_pair, 0)
    for u in range(UNROLL):
        source[live + u] = 48
        owner[live + u] = 0

    for level in range(5):
        per = 16 >> level

        def list_far(t, carry, level=level, per=per):
            i = OFFSETS[level] + t // 8
            rel = far_inner[i, t % 8] - (leaf - 1) * per
            table[i * 8 + t % 8] = (rel // per) * NODES + OFFSETS[level] + rel % per
            return carry

        lax.fori_loop(0, per * 8, list_far, 0)
    for level in range(3):
        for f in range(8):
            table[(NODES + level) * 8 + f] = 3 * NODES + level * 8 + f

    def pack(dst, at, coords, loads):
        dst[at, 0:32] = coords
        dst[at, 32:48] = extra_rows(coords, False).astype(BF16)
        dst[at, 48:80] = loads

    for tree, (p, c) in enumerate(
        ((side_points.at[0], side_charges.at[0]), (points, charges), (side_points.at[1], side_charges.at[1]))
    ):
        for i in range(16):
            cols = slice(i * 256, (i + 1) * 256)
            pack(leaf_block, tree * 16 + i, p[:, cols], c[:, cols])
    leaf_block[48] = jnp.zeros((80, 256), BF16)

    for tree, ref in enumerate((side_nodes.at[0], nodes, side_nodes.at[1])):

        def pack_node(n, carry, tree=tree, ref=ref):
            value = ref[n]
            pack(node_block, tree * NODES + n, value[:32], value[32:])
            return carry

        lax.fori_loop(0, NODES, pack_node, 0)

    def pack_upper(f, carry):
        low, high = chosen[0, f], chosen[1, f]
        coords = jnp.concatenate([low[:16], high[:16]], axis=0)
        loads = jnp.concatenate([low[16:], high[16:]], axis=0)
        pack(node_block, 3 * NODES + f, coords, loads)
        return carry

    lax.fori_loop(0, 24, pack_upper, 0)

    for i in range(16):
        leaf_turned[i] = turned(points[:, i * 256 : (i + 1) * 256])

    def turn_node(n, carry):
        node_turned[n] = turned(nodes[n, :32])
        return carry

    lax.fori_loop(0, NODES, turn_node, 0)
    for level in range(3):
        node_turned[NODES + level] = turned(own_upper[level])

    near_sum[...] = jnp.zeros_like(near_sum)

    def near_step(step, carry):
        results = []
        for u in range(UNROLL):
            s = source[step * UNROLL + u]
            o = owner[step * UNROLL + u]
            coords = leaf_block[s, 0:48]
            loads = leaf_block[s, 48:80]
            parts = []
            for half in range(2):
                target = leaf_turned[o, half * 128 : (half + 1) * 128, 0:48]
                kernel = jnp.exp2(dot(target, coords) * RATE).astype(BF16)
                parts.append(dot_nt(loads, kernel))
            results.append((o, parts))
        for o, parts in results:
            for half in range(2):
                near_sum[o, :, half * 128 : (half + 1) * 128] += parts[half]
        return carry

    lax.fori_loop(0, (live + UNROLL - 1) // UNROLL, near_step, 0)

    def far_step(n, carry):
        target = node_turned[n, :, 0:48]
        total = jnp.zeros((32, 128), F32)
        for f in range(0, 8, 2):
            a, b = table[n * 8 + f], table[n * 8 + f + 1]
            coords = jnp.concatenate([node_block[a, 0:48], node_block[b, 0:48]], axis=1)
            loads = jnp.concatenate([node_block[a, 48:80], node_block[b, 48:80]], axis=1)
            kernel = jnp.exp2(dot(target, coords) * RATE).astype(BF16)
            total += dot_nt(loads, kernel)
        far_sum[n] = total
        return carry

    lax.fori_loop(0, NODES + 3, far_step, 0)

    def spread(total, mat):
        high = total.astype(BF16)
        low = (total - high.astype(F32)).astype(BF16)
        both = dot(jnp.concatenate([high, low], axis=0), mat)
        return both[:32] + both[32:]

    mat = jnp.concatenate([all7[n] for n in range(8)], axis=0)
    down = spread(far_sum[NODES + 2], mat)
    down = jnp.where((g // 4) % 2 == 1, down[:, 128:], down[:, :128])
    mat = jnp.concatenate([all6[4 * (g // 4) + n] for n in range(4)], axis=0)
    down = spread(far_sum[NODES + 1] + down, mat)
    down = jnp.where((g // 2) % 2 == 1, down[:, 128:], down[:, :128])
    mat = jnp.concatenate([all5[2 * (g // 2) + n] for n in range(2)], axis=0)
    down = spread(far_sum[NODES] + down, mat)
    down = jnp.where(g % 2 == 1, down[:, 128:], down[:, :128])
    totals = [far_sum[30] + down]
    for level in range(4, 0, -1):
        children = []
        for i, total in enumerate(totals):
            both = spread(total, inner_maps[OFFSETS[level] - 16 + i])
            for side in range(2):
                child = OFFSETS[level - 1] + 2 * i + side
                children.append(far_sum[child] + both[:, side * 128 : (side + 1) * 128])
        totals = children
    for i, total in enumerate(totals):
        value = near_sum[i] + spread(total, leaf_maps[i])
        out[i // 4, :, (i % 4) * 256 : (i % 4 + 1) * 256] = value.astype(BF16)


def sum_kernel(parts, out, arrived, send_sem, recv_sem):
    leaf = lax.axis_index("leaf")
    plane = lax.axis_index("list")
    barrier = pltpu.get_barrier_semaphore()
    others = [(plane + k) % 4 for k in range(1, 4)]
    for who in others:
        pl.semaphore_signal(barrier, inc=1, device_id=(leaf, who), device_id_type=MESH)
    pl.semaphore_wait(barrier, 3)
    copies = []
    for n, who in enumerate(others):
        copy = pltpu.make_async_remote_copy(
            src_ref=parts.at[who], dst_ref=arrived.at[n], send_sem=send_sem.at[n],
            recv_sem=recv_sem.at[n], device_id=(leaf, who), device_id_type=MESH,
        )
        copy.start()
        copies.append(copy)
    total = parts[plane].astype(F32)
    for n, copy in enumerate(copies):
        copy.wait_recv()
        total += arrived[n].astype(F32)
    out[...] = total
    for copy in copies:
        copy.wait_send()


def on_device(
    points, charges, leaf_ids, inner_ids, upper_ids_first, upper_ids_second, upper_ids_third,
    leaf_maps, inner_maps, upper_maps_first, upper_maps_second, upper_maps_third,
    near_lists, far_inner, far_upper_first, far_upper_second, far_upper_third,
):
    def shape(*dims, kind=BF16):
        return jax.ShapeDtypeStruct(dims, kind)

    dma = pltpu.SemaphoreType.DMA
    (side_points, side_charges, nodes, side_nodes, all5, all6, all7, near_all, own_upper, chosen) = pl.pallas_call(
        gather_kernel,
        out_shape=[
            shape(2, 32, 4096), shape(2, 32, 4096), shape(NODES, 64, 128), shape(2, NODES, 64, 128),
            shape(8, 64, 256), shape(8, 32, 256), shape(8, 16, 256), shape(4, 16, 8, kind=jnp.int32),
            shape(3, 32, 128), shape(2, 24, 32, 128),
        ],
        in_specs=[VMEM] * 13 + [SMEM] * 3,
        out_specs=[VMEM] * 10,
        scratch_shapes=[
            pltpu.VMEM((8, 64, 128), BF16), pltpu.VMEM((4, 64, 128), BF16), pltpu.VMEM((2, 64, 128), BF16),
            pltpu.VMEM((1, 64, 128), BF16), pltpu.VMEM((32, 128), BF16), pltpu.VMEM((32, 128), BF16),
            pltpu.VMEM((32, 128), BF16), pltpu.VMEM((24, 32, 128), BF16),
            pltpu.VMEM((64, 32, 128), BF16), pltpu.VMEM((32, 32, 128), BF16), pltpu.VMEM((16, 32, 128), BF16),
            dma((3, 8)), dma((3, 8)), dma((4,)), dma((4,)), dma((8,)), dma((8,)), dma((2, 3)), dma((2, 3)),
            dma((2, 3, 8)), dma((2, 3, 8)), dma, dma,
        ],
        compiler_params=pltpu.CompilerParams(collective_id=0, has_side_effects=True),
        name="gather_nodes",
    )(
        points, charges, leaf_ids, inner_ids, upper_ids_first, upper_ids_second, upper_ids_third,
        leaf_maps, inner_maps, upper_maps_first, upper_maps_second, upper_maps_third, near_lists,
        far_upper_first, far_upper_second, far_upper_third,
    )
    parts = pl.pallas_call(
        field_kernel,
        out_shape=shape(4, 32, 1024),
        in_specs=[VMEM] * 13 + [SMEM] * 2,
        out_specs=VMEM,
        scratch_shapes=[
            pltpu.VMEM((49, 80, 256), BF16), pltpu.VMEM((3 * NODES + 24, 80, 128), BF16),
            pltpu.VMEM((16, 256, 128), BF16), pltpu.VMEM((NODES + 3, 128, 128), BF16),
            pltpu.VMEM((16, 32, 256), F32), pltpu.VMEM((NODES + 3, 32, 128), F32),
            pltpu.SMEM((128 + UNROLL,), jnp.int32), pltpu.SMEM((128 + UNROLL,), jnp.int32),
            pltpu.SMEM(((NODES + 3) * 8,), jnp.int32),
        ],
        name="fields",
    )(
        points, charges, side_points, side_charges, nodes, side_nodes, all5, all6, all7, own_upper, chosen,
        inner_maps, leaf_maps, near_all.reshape(64, 8), far_inner,
    )
    return pl.pallas_call(
        sum_kernel,
        out_shape=shape(32, 1024, kind=F32),
        in_specs=[VMEM],
        out_specs=VMEM,
        scratch_shapes=[pltpu.VMEM((3, 32, 1024), BF16), dma((3,)), dma((3,))],
        compiler_params=pltpu.CompilerParams(collective_id=1, has_side_effects=True),
        name="sum_lists",
    )(parts)


def solution(mesh):
    placed = (
        P(None, "leaf"), P(None, "leaf"), P("leaf", None), P("leaf", None), P(), P(), P(),
        P("leaf", None, None), P("leaf", None, None), P("leaf", None), P("leaf", None), P("leaf", None),
        P("leaf", "list"), P("leaf", "list"), P(None, "list"), P(None, "list"), P(None, "list"),
    )
    return jax.shard_map(
        on_device, mesh=mesh, in_specs=placed, out_specs=P(None, ("leaf", "list")), check_vma=False
    )
```

```python
import math

import jax
import jax.numpy as jnp
from jax import lax
from jax.experimental import pallas as pl
from jax.experimental.pallas import tpu as pltpu
from jax.sharding import PartitionSpec as P

MESH = pl.DeviceIdType.MESH
BF16 = jnp.bfloat16
F32 = jnp.float32
VMEM = pl.BlockSpec(memory_space=pltpu.VMEM)
SMEM = pl.BlockSpec(memory_space=pltpu.SMEM)
NODES = 31
OFFSETS = (0, 16, 24, 28, 30)
RATE = -3.0 / 32.0 * math.log2(math.e)
NT = (((1,), (1,)), ((), ()))


def dot(a, b):
    return jnp.dot(a, b, preferred_element_type=F32)


def dot_nt(a, b):
    return lax.dot_general(a, b, NT, preferred_element_type=F32)


def climb(coords, weights, ids, mat):
    rows = lax.broadcasted_iota(jnp.int32, (256, 128), 0)
    hot = jnp.where(rows == ids, 1.0, 0.0).astype(BF16)
    return dot(coords, hot).astype(BF16), dot_nt(weights, mat).astype(BF16)


def extra_rows(coords, target):
    wide = coords.astype(F32)
    norm = jnp.sum(wide * wide, axis=0, keepdims=True)
    high = norm.astype(BF16).astype(F32)
    rest = norm - high
    middle = rest.astype(BF16).astype(F32)
    low = (rest - middle).astype(BF16).astype(F32)
    shape = (16, coords.shape[1])
    row = lax.broadcasted_iota(jnp.int32, shape, 0)
    at, ones = (3, 0) if target else (0, 3)
    out = jnp.where((row >= ones) & (row < ones + 3), 1.0, 0.0)
    for n, part in enumerate((high, middle, low)):
        out = jnp.where(row == at + n, jnp.broadcast_to(part, shape), out)
    return out


def turned(coords):
    width = coords.shape[1]
    rows = [-2.0 * coords.astype(F32), extra_rows(coords, True), jnp.zeros((80, width), F32)]
    return jnp.concatenate(rows, axis=0).T.astype(BF16)


def pack(dst, at, coords, loads):
    dst[at, 0:32] = coords
    dst[at, 32:48] = extra_rows(coords, False).astype(BF16)
    dst[at, 48:80] = loads


def spread(total, mat):
    high = total.astype(BF16)
    low = (total - high.astype(F32)).astype(BF16)
    both = dot(jnp.concatenate([high, low], axis=0), mat)
    return both[:32] + both[32:]


def fields(jobs):
    totals = []
    waiting = None
    for n, (target, blocks) in enumerate(jobs):
        totals.append(None)
        for coords, loads in blocks:
            distance = dot(target, coords)
            if waiting is not None:
                at, kernel, held = waiting
                term = dot_nt(held, kernel)
                totals[at] = term if totals[at] is None else totals[at] + term
            waiting = (n, jnp.exp2(distance * RATE).astype(BF16), loads)
    at, kernel, held = waiting
    term = dot_nt(held, kernel)
    totals[at] = term if totals[at] is None else totals[at] + term
    return totals


def whole_kernel(
    points, charges, leaf_ids, inner_ids, ids5, ids6, ids7, leaf_maps, inner_maps,
    maps5, maps6, maps7, near, far_inner, far5, far6, far7,
    out,
    leaf_block, node_block, leaf_turned, node_turned, near_sum, far_sum, totals,
    all5, all6, all7, roots, group5, group6, group7, half5, half6, half7, buf5, buf6, buf7, chosen,
    parts, arrived,
    map_send, map_recv, root_send, root_recv, side_send, side_recv, spread_send, spread_recv,
    ring_send, ring_recv, swap_send, swap_recv, sum_send, sum_recv,
):
    leaf = lax.axis_index("leaf")
    plane = lax.axis_index("list")
    core = leaf % 2
    y = (leaf // 2) % 8
    z = leaf // 16
    g = leaf % 8
    quad = leaf // 8
    outer = (leaf + 127 + 2 * core) % 128
    sibling = leaf + 1 - 2 * core
    group = [quad * 8 + (g + k) % 8 for k in range(1, 8)]
    row = [z * 16 + ((y + k) % 8) * 2 + core for k in range(1, 8)]
    column = [((z + k) % 8) * 16 + y * 2 + core for k in range(1, 8)]
    planes = [(leaf, (plane + k) % 4) for k in range(1, 4)]

    def to(who):
        return (who, plane)

    barrier = pltpu.get_barrier_semaphore()
    peers = [to(w) for w in (outer, sibling, *group, *row, *column)] + planes
    for who in peers:
        pl.semaphore_signal(barrier, inc=1, device_id=who, device_id_type=MESH)

    for i in range(16):
        cols = slice(i * 256, (i + 1) * 256)
        pack(leaf_block, 16 + i, points[:, cols], charges[:, cols])
    leaf_block[48] = jnp.zeros((80, 256), BF16)

    pl.semaphore_wait(barrier, len(peers))

    def remote(src, dst, s_sem, r_sem, who):
        return pltpu.make_async_remote_copy(
            src_ref=src, dst_ref=dst, send_sem=s_sem, recv_sem=r_sem, device_id=who, device_id_type=MESH
        )

    def start(copies):
        for copy in copies:
            copy.start()
        return copies

    def arrive(copies):
        for copy in copies:
            copy.wait_recv()

    levels = ((maps5, all5), (maps6, all6), (maps7, all7))
    map_same = []
    for k in (2, 4, 6, 0):
        who = sibling if k == 0 else group[k - 1]
        for n, (src, dst) in enumerate(levels):
            map_same.append(remote(src, dst.at[g], map_send.at[n, k], map_recv.at[n, k], to(who)))
    start(map_same)

    def side(n, block, stride, quarter):
        own = stride
        to_sibling = remote(
            block.at[pl.ds(own, stride)], block.at[pl.ds(2 * core * stride, stride)],
            side_send.at[n, 0], side_recv.at[n, 0], to(sibling),
        )
        to_outer = remote(
            block.at[pl.ds(own + plane * quarter, quarter)],
            block.at[pl.ds(2 * (1 - core) * stride + plane * quarter, quarter)],
            side_send.at[n, 1], side_recv.at[n, 1], to(outer),
        )
        piece = block.at[pl.ds(2 * core * stride + plane * quarter, quarter)]
        to_planes = [
            remote(piece, piece, spread_send.at[n, k], spread_recv.at[n, k], planes[k]) for k in range(3)
        ]
        return to_sibling, to_outer, to_planes

    leaf_sibling, leaf_outer, leaf_planes = side(0, leaf_block, 16, 4)
    node_sibling, node_outer, node_planes = side(1, node_block, 32, 8)
    start([leaf_outer, leaf_sibling])
    all5[g] = maps5[...]
    all6[g] = maps6[...]
    all7[g] = maps7[...]

    for i in range(16):
        cols = slice(i * 256, (i + 1) * 256)
        pack(
            node_block, 32 + i,
            *climb(points[:, cols], charges[:, cols], leaf_ids[i : i + 1, :], leaf_maps[i]),
        )
    leaf_outer.wait_recv()
    start(leaf_planes)
    for level in range(1, 5):
        for i in range(16 >> level):
            child = 32 + OFFSETS[level - 1] + 2 * i
            n = OFFSETS[level] - 16 + i
            coords = jnp.concatenate([node_block[child, 0:32], node_block[child + 1, 0:32]], axis=1)
            loads = jnp.concatenate([node_block[child, 48:80], node_block[child + 1, 48:80]], axis=1)
            pack(node_block, 48 + n, *climb(coords, loads, inner_ids[n : n + 1, :], inner_maps[n]))
    node_block[63] = jnp.zeros((80, 128), BF16)
    roots[g, :32] = node_block[62, 0:32]
    roots[g, 32:] = node_block[62, 48:80]

    root_copies = start(
        [
            remote(roots.at[g], roots.at[g], root_send.at[k], root_recv.at[k], to(group[k - 1]))
            for k in range(1, 8)
        ]
    )
    start([node_outer, node_sibling])

    map_over = []
    for k in (2, 4, 6):
        for n, (_src, dst) in enumerate(levels):
            slot = dst.at[(g + 8 - k) % 8]
            map_over.append(remote(slot, slot, map_send.at[n, k - 1], map_recv.at[n, k - 1], to(sibling)))
    arrive(map_same)
    start(map_over)

    for i in range(16):
        leaf_turned[i] = turned(points[:, i * 256 : (i + 1) * 256])
    for i in range(NODES):
        node_turned[i] = turned(node_block[32 + i, 0:32])

    arrive(map_over + root_copies)

    def keep(dst, j, coords, weights):
        dst[j, :32] = coords
        dst[j, 32:] = weights

    def join(src, j):
        both = jnp.concatenate([src[2 * j], src[2 * j + 1]], axis=1)
        return both[:32], both[32:]

    for j in range(4):
        mat = jnp.concatenate([all5[2 * j], all5[2 * j + 1]], axis=0)
        keep(group5, j, *climb(*join(roots, j), ids5[pl.ds(quad * 4 + j, 1), :], mat))
    for j in range(2):
        mat = jnp.concatenate([all6[4 * j + n] for n in range(4)], axis=0)
        keep(group6, j, *climb(*join(group5, j), ids6[pl.ds(quad * 2 + j, 1), :], mat))
    mat = jnp.concatenate([all7[n] for n in range(8)], axis=0)
    keep(group7, 0, *climb(*join(group6, 0), ids7[pl.ds(quad, 1), :], mat))

    mine = (group5[g // 2], group6[g // 4], group7[0])
    halves = (half5, half6, half7)
    bufs = (buf5, buf6, buf7)
    some = (range(1, 8), (2, 4, 6), (4,))
    every = (range(1, 8),) * 3

    def ring(c, stages):
        if c == 0:
            slots = (leaf // 2, leaf // 4, leaf // 8)
            slabs = [bufs[n].at[pl.ds(z * (8 >> n), 8 >> n)] for n in range(3)]
            plan = ((some, row), (every, column))
        else:
            slots = (y * 8 + z, (y // 2) * 8 + z, (y // 4) * 8 + z)
            slabs = [bufs[n].at[pl.ds((y // (1 << n)) * 8, 8)] for n in range(3)]
            plan = ((every, column), (some, row))
        ways = []
        for stage in range(stages):
            steps, line = plan[stage]
            ways.append(
                [
                    [
                        remote(
                            slabs[n] if stage else halves[n], slabs[n] if stage else bufs[n].at[slots[n]],
                            ring_send.at[stage, n, k], ring_recv.at[stage, n, k], to(line[k - 1]),
                        )
                        for k in steps[n]
                    ]
                    for n in range(3)
                ]
            )
        return slots, ways

    def first_stage(c):
        for n in range(3):
            halves[n][:16] = mine[n][16 * c : 16 * c + 16]
            halves[n][16:] = mine[n][32 + 16 * c : 48 + 16 * c]
        slots, (first,) = ring(c, 1)
        for n in range(3):
            start(first[n])
            bufs[n][slots[n]] = halves[n][...]

    def second_stage(c):
        _, (first, second) = ring(c, 2)
        for n in range(3):
            arrive(first[n])
            start(second[n])

    def end_stage(c):
        _, (first, second) = ring(c, 2)
        for n in range(3):
            arrive(second[n])
            for copy in first[n] + second[n]:
                copy.wait_send()

    def by_core(body):
        for c in range(2):
            pl.when(core == c)(lambda c=c: body(c))

    by_core(first_stage)
    for n in range(3):
        node_turned[NODES + n] = turned(mine[n][:32])
    node_outer.wait_recv()
    start(node_planes)

    def near_step(step, carry):
        jobs = []
        for a in range(4):
            i = step * 4 + a
            blocks = []
            for f in range(8):
                entry = near[f, i]
                s = jnp.where(entry >= 0, jnp.clip(entry - (leaf - 1) * 16, 0, 47), 48)
                blocks.append((leaf_block[s, 0:48], leaf_block[s, 48:80]))
            jobs.append((leaf_turned[i, :, 0:48], blocks))
        for a, total in enumerate(fields(jobs)):
            near_sum[step * 4 + a] = total
        return carry

    arrive([leaf_sibling] + leaf_planes)
    lax.fori_loop(0, 2, near_step, 0)
    by_core(second_stage)
    lax.fori_loop(2, 4, near_step, 0)

    def far_job(i, index):
        blocks = []
        for f in range(0, 8, 4):
            at = [index(f + n) for n in range(4)]
            blocks.append(
                (
                    jnp.concatenate([node_block[a, 0:48] for a in at], axis=1),
                    jnp.concatenate([node_block[a, 48:80] for a in at], axis=1),
                )
            )
        return node_turned[i, :, 0:48], blocks

    def inner_job(level, i):
        per = 16 >> level

        def index(f):
            rel = jnp.clip(far_inner[f, OFFSETS[level] + i] - (leaf - 1) * per, 0, 3 * per - 1)
            return (rel // per) * 32 + OFFSETS[level] + rel % per

        return far_job(OFFSETS[level] + i, index)

    arrive([node_sibling] + node_planes)
    for level in range(3):

        def far_step(step, carry, level=level):
            jobs = [inner_job(level, step * 4 + a) for a in range(4)]
            for a, total in enumerate(fields(jobs)):
                far_sum[OFFSETS[level] + step * 4 + a] = total
            return carry

        lax.fori_loop(0, 4 >> level, far_step, 0)
    for n, total in enumerate(fields([inner_job(3, 0), inner_job(3, 1), inner_job(4, 0)])):
        far_sum[28 + n] = total

    by_core(end_stage)
    for f in range(8):
        n5 = jnp.clip(far5[f, leaf // 2], 0, 63)
        n6 = jnp.clip(far6[f, leaf // 4], 0, 31)
        n7 = jnp.clip(far7[f, leaf // 8], 0, 15)
        chosen[core, f] = buf5[(1 - core) * n5 + core * ((n5 % 8) * 8 + n5 // 8)]
        chosen[core, 8 + f] = buf6[(1 - core) * n6 + core * ((n6 % 4) * 8 + n6 // 4)]
        chosen[core, 16 + f] = buf7[(1 - core) * n7 + core * ((n7 % 2) * 8 + n7 // 2)]
    swap = remote(chosen.at[core], chosen.at[core], swap_send, swap_recv, to(sibling))
    swap.start()
    swap.wait_recv()
    for f in range(24):
        low, high = chosen[0, f], chosen[1, f]
        coords = jnp.concatenate([low[:16], high[:16]], axis=0)
        pack(node_block, 96 + f, coords, jnp.concatenate([low[16:], high[16:]], axis=0))
    upper = fields([far_job(NODES + n, lambda f, n=n: 96 + n * 8 + f) for n in range(3)])

    def half_of(value, bit):
        return jnp.where(bit % 2 == 1, value[:, 128:], value[:, :128])

    mat = jnp.concatenate([all7[n] for n in range(8)], axis=0)
    down = half_of(spread(upper[2], mat), g // 4)
    mat = jnp.concatenate([all6[4 * (g // 4) + n] for n in range(4)], axis=0)
    down = half_of(spread(upper[1] + down, mat), g // 2)
    mat = jnp.concatenate([all5[2 * (g // 2) + n] for n in range(2)], axis=0)
    down = half_of(spread(upper[0] + down, mat), g)
    here = [far_sum[30] + down]
    for level in range(4, 0, -1):
        children = []
        for i, total in enumerate(here):
            both = spread(total, inner_maps[OFFSETS[level] - 16 + i])
            for n in range(2):
                child = OFFSETS[level - 1] + 2 * i + n
                children.append(far_sum[child] + both[:, n * 128 : (n + 1) * 128])
        here = children
    for i in range(16):
        totals[i] = here[i]

    sums = []
    for k in (2, 1, 3, 0):
        quarter = (plane + k) % 4
        for j in range(4):
            i = quarter * 4 + j
            value = near_sum[i] + spread(totals[i], leaf_maps[i])
            if k == 0:
                out[:, j * 256 : (j + 1) * 256] = value
            else:
                parts[k - 1, :, j * 256 : (j + 1) * 256] = value.astype(BF16)
        if k:
            sums += start(
                [remote(parts.at[k - 1], arrived.at[k - 1], sum_send.at[k], sum_recv.at[k], planes[k - 1])]
            )
    arrive(sums)
    out[...] += arrived[0].astype(F32) + arrived[1].astype(F32) + arrived[2].astype(F32)
    ended = map_same + map_over + root_copies + leaf_planes + node_planes + sums
    for copy in ended + [leaf_sibling, leaf_outer, node_sibling, node_outer, swap]:
        copy.wait_send()


def on_device(
    points, charges, leaf_ids, inner_ids, upper_ids_first, upper_ids_second, upper_ids_third,
    leaf_maps, inner_maps, upper_maps_first, upper_maps_second, upper_maps_third,
    near_lists, far_inner, far_upper_first, far_upper_second, far_upper_third,
):
    dma = pltpu.SemaphoreType.DMA

    def room(*dims, kind=BF16):
        return pltpu.VMEM(dims, kind)

    return pl.pallas_call(
        whole_kernel,
        out_shape=jax.ShapeDtypeStruct((32, 1024), F32),
        in_specs=[VMEM] * 12 + [SMEM] * 5,
        out_specs=VMEM,
        scratch_shapes=[
            room(49, 80, 256), room(96 + 24, 80, 128), room(16, 256, 128), room(NODES + 3, 128, 128),
            room(16, 32, 256, kind=F32), room(NODES, 32, 128, kind=F32), room(16, 32, 128, kind=F32),
            room(8, 64, 256), room(8, 32, 256), room(8, 16, 256),
            room(8, 64, 128), room(4, 64, 128), room(2, 64, 128), room(1, 64, 128),
            room(32, 128), room(32, 128), room(32, 128),
            room(64, 32, 128), room(32, 32, 128), room(16, 32, 128), room(2, 24, 32, 128),
            room(3, 32, 1024), room(3, 32, 1024),
            dma((3, 8)), dma((3, 8)), dma((8,)), dma((8,)), dma((2, 2)), dma((2, 2)), dma((2, 3)), dma((2, 3)),
            dma((2, 3, 8)), dma((2, 3, 8)), dma, dma, dma((4,)), dma((4,)),
        ],
        compiler_params=pltpu.CompilerParams(collective_id=0, has_side_effects=True),
        name="tree_product",
    )(
        points, charges, leaf_ids, inner_ids, upper_ids_first, upper_ids_second, upper_ids_third,
        leaf_maps, inner_maps, upper_maps_first, upper_maps_second, upper_maps_third,
        near_lists.T, far_inner.T, far_upper_first.T, far_upper_second.T, far_upper_third.T,
    )


def solution(mesh):
    placed = (
        P(None, "leaf"), P(None, "leaf"), P("leaf", None), P("leaf", None), P(), P(), P(),
        P("leaf", None, None), P("leaf", None, None), P("leaf", None), P("leaf", None), P("leaf", None),
        P("leaf", "list"), P("leaf", "list"), P(None, "list"), P(None, "list"), P(None, "list"),
    )
    return jax.shard_map(
        on_device, mesh=mesh, in_specs=placed, out_specs=P(None, ("leaf", "list")), check_vma=False
    )
```

```python
import math

import jax
import jax.numpy as jnp
from jax import lax
from jax.experimental import pallas as pl
from jax.experimental.pallas import tpu as pltpu
from jax.sharding import PartitionSpec as P

MESH = pl.DeviceIdType.MESH
BF16 = jnp.bfloat16
F32 = jnp.float32
VMEM = pl.BlockSpec(memory_space=pltpu.VMEM)
SMEM = pl.BlockSpec(memory_space=pltpu.SMEM)
NODES = 31
OFFSETS = (0, 16, 24, 28, 30)
RATE = -3.0 / 32.0 * math.log2(math.e)
NT = (((1,), (1,)), ((), ()))


def dot(a, b):
    return jnp.dot(a, b, preferred_element_type=F32)


def dot_nt(a, b):
    return lax.dot_general(a, b, NT, preferred_element_type=F32)


def climb(coords, weights, ids, mat):
    rows = lax.broadcasted_iota(jnp.int32, (256, 128), 0)
    hot = jnp.where(rows == ids, 1.0, 0.0).astype(BF16)
    return dot(coords, hot).astype(BF16), dot_nt(weights, mat).astype(BF16)


def extra_rows(coords, target):
    wide = coords.astype(F32)
    norm = jnp.sum(wide * wide, axis=0, keepdims=True)
    high = norm.astype(BF16).astype(F32)
    rest = norm - high
    middle = rest.astype(BF16).astype(F32)
    low = (rest - middle).astype(BF16).astype(F32)
    shape = (16, coords.shape[1])
    row = lax.broadcasted_iota(jnp.int32, shape, 0)
    at, ones = (3, 0) if target else (0, 3)
    out = jnp.where((row >= ones) & (row < ones + 3), 1.0, 0.0)
    for n, part in enumerate((high, middle, low)):
        out = jnp.where(row == at + n, jnp.broadcast_to(part, shape), out)
    return out


def turned(coords):
    rows = [-2.0 * coords.astype(F32), extra_rows(coords, True)]
    return jnp.concatenate(rows, axis=0).T.astype(BF16)


def pack(dst, at, coords, loads):
    dst[at, 0:32] = coords
    dst[at, 32:48] = extra_rows(coords, False).astype(BF16)
    dst[at, 48:80] = loads


def spread(total, mat):
    high = total.astype(BF16)
    low = (total - high.astype(F32)).astype(BF16)
    both = dot(jnp.concatenate([high, low], axis=0), mat)
    return both[:32] + both[32:]


def fields(jobs):
    totals = []
    waiting = None
    for n, (target, blocks) in enumerate(jobs):
        totals.append(None)
        for coords, loads in blocks:
            distance = dot(target, coords)
            if waiting is not None:
                at, kernel, held = waiting
                term = dot_nt(held, kernel)
                totals[at] = term if totals[at] is None else totals[at] + term
            waiting = (n, jnp.exp2(distance * RATE).astype(BF16), loads)
    at, kernel, held = waiting
    term = dot_nt(held, kernel)
    totals[at] = term if totals[at] is None else totals[at] + term
    return totals


def whole_kernel(
    points, charges, leaf_ids, inner_ids, ids5, ids6, ids7, leaf_maps_far, inner_maps_far,
    maps5, maps6, maps7, near, far_inner, far5, far6, far7,
    out,
    leaf_block, node_block, leaf_turned, node_turned, near_sum, far_sum, totals,
    all5, all6, all7, roots, group5, group6, group7, half5, half6, half7, buf5, buf6, buf7, chosen,
    parts, arrived, leaf_maps, inner_maps, fetched,
    map_send, map_recv, root_send, root_recv, side_send, side_recv, spread_send, spread_recv,
    ring_send, ring_recv, swap_send, swap_recv, sum_send, sum_recv,
):
    fetches = [
        pltpu.make_async_copy(leaf_maps_far, leaf_maps, fetched.at[0]),
        pltpu.make_async_copy(inner_maps_far, inner_maps, fetched.at[1]),
    ]
    for fetch in fetches:
        fetch.start()
    leaf = lax.axis_index("leaf")
    plane = lax.axis_index("list")
    core = leaf % 2
    y = (leaf // 2) % 8
    z = leaf // 16
    g = leaf % 8
    quad = leaf // 8
    outer = (leaf + 127 + 2 * core) % 128
    sibling = leaf + 1 - 2 * core
    group = [quad * 8 + (g + k) % 8 for k in range(1, 8)]
    row = [z * 16 + ((y + k) % 8) * 2 + core for k in range(1, 8)]
    column = [((z + k) % 8) * 16 + y * 2 + core for k in range(1, 8)]
    planes = [(leaf, (plane + k) % 4) for k in range(1, 4)]

    def to(who):
        return (who, plane)

    barrier = pltpu.get_barrier_semaphore()
    peers = [to(w) for w in (outer, sibling, *group, *row, *column)] + planes
    for who in peers:
        pl.semaphore_signal(barrier, inc=1, device_id=who, device_id_type=MESH)

    pl.semaphore_wait(barrier, len(peers))

    def remote(src, dst, s_sem, r_sem, who):
        return pltpu.make_async_remote_copy(
            src_ref=src, dst_ref=dst, send_sem=s_sem, recv_sem=r_sem, device_id=who, device_id_type=MESH
        )

    def start(copies):
        for copy in copies:
            copy.start()
        return copies

    def arrive(copies):
        for copy in copies:
            copy.wait_recv()

    levels = ((maps5, all5), (maps6, all6), (maps7, all7))
    map_same = []
    for k in (2, 4, 6, 0):
        who = sibling if k == 0 else group[k - 1]
        for n, (src, dst) in enumerate(levels):
            map_same.append(remote(src, dst.at[g], map_send.at[n, k], map_recv.at[n, k], to(who)))
    start(map_same)

    def side(n, block, stride, quarter):
        own = stride
        to_sibling = remote(
            block.at[pl.ds(own, stride)], block.at[pl.ds(2 * core * stride, stride)],
            side_send.at[n, 0], side_recv.at[n, 0], to(sibling),
        )
        to_outer = []
        for k in range(2):
            at = ((plane + 2 * k) % 4) * quarter
            to_outer.append(
                remote(
                    block.at[pl.ds(own + at, quarter)],
                    block.at[pl.ds(2 * (1 - core) * stride + at, quarter)],
                    side_send.at[n, 1 + k], side_recv.at[n, 1 + k], to(outer),
                )
            )
        piece = block.at[pl.ds(2 * core * stride + plane * quarter, quarter)]
        to_planes = [
            remote(piece, piece, spread_send.at[n, k], spread_recv.at[n, k], planes[2 * k]) for k in range(2)
        ]
        return to_sibling, to_outer, to_planes

    leaf_sibling, leaf_outer, leaf_planes = side(0, leaf_block, 16, 4)
    node_sibling, node_outer, node_planes = side(1, node_block, 32, 8)
    for i in range(16):
        cols = slice(i * 256, (i + 1) * 256)
        pack(leaf_block, 16 + i, points[:, cols], charges[:, cols])
    leaf_block[48] = jnp.zeros((80, 256), BF16)
    start(leaf_outer + [leaf_sibling])
    all5[g] = maps5[...]
    all6[g] = maps6[...]
    all7[g] = maps7[...]

    fetches[0].wait()
    for i in range(16):
        cols = slice(i * 256, (i + 1) * 256)
        pack(
            node_block, 32 + i,
            *climb(points[:, cols], charges[:, cols], leaf_ids[i : i + 1, :], leaf_maps[i]),
        )
    fetches[1].wait()
    for level in range(1, 5):
        for i in range(16 >> level):
            child = 32 + OFFSETS[level - 1] + 2 * i
            n = OFFSETS[level] - 16 + i
            coords = jnp.concatenate([node_block[child, 0:32], node_block[child + 1, 0:32]], axis=1)
            loads = jnp.concatenate([node_block[child, 48:80], node_block[child + 1, 48:80]], axis=1)
            pack(node_block, 48 + n, *climb(coords, loads, inner_ids[n : n + 1, :], inner_maps[n]))
    node_block[63] = jnp.zeros((80, 128), BF16)
    roots[g, :32] = node_block[62, 0:32]
    roots[g, 32:] = node_block[62, 48:80]

    root_copies = start(
        [
            remote(roots.at[g], roots.at[g], root_send.at[k], root_recv.at[k], to(group[k - 1]))
            for k in range(1, 8)
        ]
    )
    start(node_outer + [node_sibling])

    map_over = []
    for k in (2, 4, 6):
        for n, (_src, dst) in enumerate(levels):
            slot = dst.at[(g + 8 - k) % 8]
            map_over.append(remote(slot, slot, map_send.at[n, k - 1], map_recv.at[n, k - 1], to(sibling)))
    arrive(map_same)
    start(map_over)

    for i in range(16):
        leaf_turned[i, :, 0:48] = turned(points[:, i * 256 : (i + 1) * 256])
    leaf_outer[0].wait_recv()
    start(leaf_planes)

    arrive(map_over + root_copies)

    def keep(dst, j, coords, weights):
        dst[j, :32] = coords
        dst[j, 32:] = weights

    def join(src, j):
        both = jnp.concatenate([src[2 * j], src[2 * j + 1]], axis=1)
        return both[:32], both[32:]

    for j in range(4):
        mat = jnp.concatenate([all5[2 * j], all5[2 * j + 1]], axis=0)
        keep(group5, j, *climb(*join(roots, j), ids5[pl.ds(quad * 4 + j, 1), :], mat))
    for j in range(2):
        mat = jnp.concatenate([all6[4 * j + n] for n in range(4)], axis=0)
        keep(group6, j, *climb(*join(group5, j), ids6[pl.ds(quad * 2 + j, 1), :], mat))
    mat = jnp.concatenate([all7[n] for n in range(8)], axis=0)
    keep(group7, 0, *climb(*join(group6, 0), ids7[pl.ds(quad, 1), :], mat))

    mine = (group5[g // 2], group6[g // 4], group7[0])
    halves = (half5, half6, half7)
    bufs = (buf5, buf6, buf7)
    some = (range(1, 8), (2, 4, 6), (4,))
    every = (range(1, 8),) * 3

    def ring(c, stages):
        if c == 0:
            slots = (leaf // 2, leaf // 4, leaf // 8)
            slabs = [bufs[n].at[pl.ds(z * (8 >> n), 8 >> n)] for n in range(3)]
            plan = ((some, row), (every, column))
        else:
            slots = (y * 8 + z, (y // 2) * 8 + z, (y // 4) * 8 + z)
            slabs = [bufs[n].at[pl.ds((y // (1 << n)) * 8, 8)] for n in range(3)]
            plan = ((every, column), (some, row))
        ways = []
        for stage in range(stages):
            steps, line = plan[stage]
            ways.append(
                [
                    [
                        remote(
                            slabs[n] if stage else halves[n], slabs[n] if stage else bufs[n].at[slots[n]],
                            ring_send.at[stage, n, k], ring_recv.at[stage, n, k], to(line[k - 1]),
                        )
                        for k in steps[n]
                    ]
                    for n in range(3)
                ]
            )
        return slots, ways

    def first_stage(c):
        for n in range(3):
            halves[n][:16] = mine[n][16 * c : 16 * c + 16]
            halves[n][16:] = mine[n][32 + 16 * c : 48 + 16 * c]
        slots, (first,) = ring(c, 1)
        for n in range(3):
            start(first[n])
            bufs[n][slots[n]] = halves[n][...]

    def second_stage(c):
        _, (first, second) = ring(c, 2)
        for n in range(3):
            arrive(first[n])
            start(second[n])

    def end_stage(c):
        _, (first, second) = ring(c, 2)
        for n in range(3):
            arrive(second[n])

    def end_sends(c):
        _, (first, second) = ring(c, 2)
        for n in range(3):
            for copy in first[n] + second[n]:
                copy.wait_send()

    def by_core(body):
        for c in range(2):
            pl.when(core == c)(lambda c=c: body(c))

    by_core(first_stage)
    for n in range(3):
        node_turned[NODES + n, :, 0:48] = turned(mine[n][:32])
    for i in range(NODES):
        node_turned[i, :, 0:48] = turned(node_block[32 + i, 0:32])
    node_outer[0].wait_recv()
    start(node_planes)

    def near_step(step, carry):
        jobs = []
        for a in range(4):
            i = step * 4 + a
            blocks = []
            for f in range(8):
                entry = near[f, i]
                s = jnp.where(entry >= 0, jnp.clip(entry - (leaf - 1) * 16, 0, 47), 48)
                blocks.append((leaf_block[s, 0:48], leaf_block[s, 48:80]))
            jobs.append((leaf_turned[i, :, 0:48], blocks))
        for a, total in enumerate(fields(jobs)):
            near_sum[step * 4 + a] = total
        return carry

    arrive([leaf_sibling, leaf_outer[1]] + leaf_planes)
    lax.fori_loop(0, 2, near_step, 0)
    by_core(second_stage)
    lax.fori_loop(2, 4, near_step, 0)

    def far_job(i, index):
        blocks = []
        for f in range(0, 8, 4):
            at = [index(f + n) for n in range(4)]
            blocks.append(
                (
                    jnp.concatenate([node_block[a, 0:48] for a in at], axis=1),
                    jnp.concatenate([node_block[a, 48:80] for a in at], axis=1),
                )
            )
        return node_turned[i, :, 0:48], blocks

    def inner_job(level, i):
        per = 16 >> level

        def index(f):
            rel = jnp.clip(far_inner[f, OFFSETS[level] + i] - (leaf - 1) * per, 0, 3 * per - 1)
            return (rel // per) * 32 + OFFSETS[level] + rel % per

        return far_job(OFFSETS[level] + i, index)

    arrive([node_sibling, node_outer[1]] + node_planes)
    for level in range(1):

        def far_step(step, carry, level=level):
            jobs = [inner_job(level, step * 4 + a) for a in range(4)]
            for a, total in enumerate(fields(jobs)):
                far_sum[OFFSETS[level] + step * 4 + a] = total
            return carry

        lax.fori_loop(0, 4 >> level, far_step, 0)
    by_core(end_stage)
    for f in range(8):
        n5 = jnp.clip(far5[f, leaf // 2], 0, 63)
        n6 = jnp.clip(far6[f, leaf // 4], 0, 31)
        n7 = jnp.clip(far7[f, leaf // 8], 0, 15)
        chosen[core, f] = buf5[(1 - core) * n5 + core * ((n5 % 8) * 8 + n5 // 8)]
        chosen[core, 8 + f] = buf6[(1 - core) * n6 + core * ((n6 % 4) * 8 + n6 // 4)]
        chosen[core, 16 + f] = buf7[(1 - core) * n7 + core * ((n7 % 2) * 8 + n7 // 2)]
    swap = remote(chosen.at[core], chosen.at[core], swap_send, swap_recv, to(sibling))
    swap.start()
    for level in range(1, 3):

        def far_step(step, carry, level=level):
            jobs = [inner_job(level, step * 4 + a) for a in range(4)]
            for a, total in enumerate(fields(jobs)):
                far_sum[OFFSETS[level] + step * 4 + a] = total
            return carry

        lax.fori_loop(0, 4 >> level, far_step, 0)
    for n, total in enumerate(fields([inner_job(3, 0), inner_job(3, 1), inner_job(4, 0)])):
        far_sum[28 + n] = total

    swap.wait_recv()
    for f in range(24):
        low, high = chosen[0, f], chosen[1, f]
        coords = jnp.concatenate([low[:16], high[:16]], axis=0)
        pack(node_block, 96 + f, coords, jnp.concatenate([low[16:], high[16:]], axis=0))
    upper = fields([far_job(NODES + n, lambda f, n=n: 96 + n * 8 + f) for n in range(3)])

    def half_of(value, bit):
        return jnp.where(bit % 2 == 1, value[:, 128:], value[:, :128])

    mat = jnp.concatenate([all7[n] for n in range(8)], axis=0)
    down = half_of(spread(upper[2], mat), g // 4)
    mat = jnp.concatenate([all6[4 * (g // 4) + n] for n in range(4)], axis=0)
    down = half_of(spread(upper[1] + down, mat), g // 2)
    mat = jnp.concatenate([all5[2 * (g // 2) + n] for n in range(2)], axis=0)
    down = half_of(spread(upper[0] + down, mat), g)
    here = [far_sum[30] + down]
    for level in range(4, 0, -1):
        children = []
        for i, total in enumerate(here):
            both = spread(total, inner_maps[OFFSETS[level] - 16 + i])
            for n in range(2):
                child = OFFSETS[level - 1] + 2 * i + n
                children.append(far_sum[child] + both[:, n * 128 : (n + 1) * 128])
        here = children
    for i in range(16):
        totals[i] = here[i]

    sums = []
    for k in (2, 1, 3, 0):
        quarter = (plane + k) % 4
        for j in range(4):
            i = quarter * 4 + j
            value = near_sum[i] + spread(totals[i], leaf_maps[i])
            if k == 0:
                out[:, j * 256 : (j + 1) * 256] = value
            else:
                parts[k - 1, :, j * 256 : (j + 1) * 256] = value.astype(BF16)
        if k:
            sums += start(
                [remote(parts.at[k - 1], arrived.at[k - 1], sum_send.at[k], sum_recv.at[k], planes[k - 1])]
            )
    arrive(sums)
    out[...] += arrived[0].astype(F32) + arrived[1].astype(F32) + arrived[2].astype(F32)
    ended = map_same + map_over + root_copies + leaf_planes + node_planes + sums
    for copy in ended + leaf_outer + node_outer + [leaf_sibling, node_sibling, swap]:
        copy.wait_send()
    by_core(end_sends)


def on_device(
    points, charges, leaf_ids, inner_ids, upper_ids_first, upper_ids_second, upper_ids_third,
    leaf_maps, inner_maps, upper_maps_first, upper_maps_second, upper_maps_third,
    near_lists, far_inner, far_upper_first, far_upper_second, far_upper_third,
):
    dma = pltpu.SemaphoreType.DMA

    def room(*dims, kind=BF16):
        return pltpu.VMEM(dims, kind)

    return pl.pallas_call(
        whole_kernel,
        out_shape=jax.ShapeDtypeStruct((32, 1024), F32),
        in_specs=[VMEM] * 7 + [pl.BlockSpec(memory_space=pl.ANY)] * 2 + [VMEM] * 3 + [SMEM] * 5,
        out_specs=VMEM,
        scratch_shapes=[
            room(49, 80, 256), room(96 + 24, 80, 128), room(16, 256, 128), room(NODES + 3, 128, 128),
            room(16, 32, 256, kind=F32), room(NODES, 32, 128, kind=F32), room(16, 32, 128, kind=F32),
            room(8, 64, 256), room(8, 32, 256), room(8, 16, 256),
            room(8, 64, 128), room(4, 64, 128), room(2, 64, 128), room(1, 64, 128),
            room(32, 128), room(32, 128), room(32, 128),
            room(64, 32, 128), room(32, 32, 128), room(16, 32, 128), room(2, 24, 32, 128),
            room(3, 32, 1024), room(3, 32, 1024), room(16, 128, 256), room(15, 128, 256), dma((2,)),
            dma((3, 8)), dma((3, 8)), dma((8,)), dma((8,)), dma((2, 3)), dma((2, 3)), dma((2, 2)), dma((2, 2)),
            dma((2, 3, 8)), dma((2, 3, 8)), dma, dma, dma((4,)), dma((4,)),
        ],
        compiler_params=pltpu.CompilerParams(collective_id=0, has_side_effects=True),
        name="tree_product",
    )(
        points, charges, leaf_ids, inner_ids, upper_ids_first, upper_ids_second, upper_ids_third,
        leaf_maps, inner_maps, upper_maps_first, upper_maps_second, upper_maps_third,
        near_lists.T, far_inner.T, far_upper_first.T, far_upper_second.T, far_upper_third.T,
    )


def solution(mesh):
    placed = (
        P(None, "leaf"), P(None, "leaf"), P("leaf", None), P("leaf", None), P(), P(), P(),
        P("leaf", None, None), P("leaf", None, None), P("leaf", None), P("leaf", None), P("leaf", None),
        P("leaf", "list"), P("leaf", "list"), P(None, "list"), P(None, "list"), P(None, "list"),
    )
    return jax.shard_map(
        on_device, mesh=mesh, in_specs=placed, out_specs=P(None, ("leaf", "list")), check_vma=False
    )
```
